128 devices in a mesh: dp: 4 (over z), seq: 32 (over y, x, core).
Axes of the slice: x: 4, y: 4, z: 4, core: 2. Of those that a mesh axis runs over, the one named last changes fastest.
Arguments:
- tokens: bfloat16 [4096, 2880], P('seq', 'dp'), may hold values from -6 to 6
- upstream: bfloat16 [4096, 2880], P('seq', 'dp'), may hold values from -6 to 6
- norm_gain: bfloat16 [2880], replicated, may hold values from 0.5 to 1.5
- experts: int32 [4096, 4], P('seq'), may hold values from 0 to 63, all different within a row; in each aligned block of 128 rows (0 to 127, 128 to 255, ...) at most 12 rows name the same one
- route_weights: bfloat16 [4096, 4], P('seq'), may hold values from 0.049804688 to 0.59765625
- w_gate_up: bfloat16 [64, 2880, 2, 1440], P('seq', None, None, 'dp'), may hold values from -0.109375 to 0.109375
- w_down: bfloat16 [64, 1440, 2880], P('seq', 'dp'), may hold values from -0.15625 to 0.15625
Outputs:
- token_gradient: bfloat16 [4096, 2880], P('seq', 'dp')
- gain_gradient: float32 [2880], P('dp')
- grad_weights: float32 [4096, 4], P('seq')
- grad_gate_up: bfloat16 [64, 2880, 2, 1440], P('seq', None, None, 'dp')
- grad_down: bfloat16 [64, 1440, 2880], P('seq', 'dp')
The draws below stay inside these ranges and needn't reach their ends.
Inputs may be any that keep to these rules, and one draw needn't show every extreme that they name: Each row names 4 different experts. In each aligned block of 128 rows (the tokens of one index of seq) no expert is named more than 12 times, a bound that some block reaches.
All inputs are finite; a program needn't handle non-finite values.
Results may differ from the reference program's by a relative error of at most 0.012.
Values may be sent and summed in bfloat16 or wider, within the bound.
No kernel may reach another device: no remote copies, remote signals or barrier semaphores. Data moves between devices by JAX's collectives and lax.ppermute only.
A program may use at most 128 MiB of HBM per device.

```python
import math
import jax
import jax.numpy as jnp
import numpy as np
from jax import lax

MODEL_WIDTH = 2880
FF = 1440
TOP = 4
TOK_DEV = 128
EXPERTS = 64
TOKENS = 4096
CAP = 12
N_SEQ = 32


def steps_of(rng, shape, shards, smallest, high):
    factor_of, own = 1.0, jax.random.fold_in(rng, 6)
    for axis_at, shards_of in shards:
        heights = jnp.exp(jax.random.uniform(jax.random.fold_in(own, axis_at), (shards_of,), jnp.float32, smallest / len(shards), high / len(shards)))
        factor_of = factor_of * jnp.repeat(heights, shape[axis_at] // shards_of).reshape([-1 if axis == axis_at else 1 for axis in range(len(shape))])
    return factor_of


def routed_block(stream_key, own, number, rows, number_of, top, bound, slope):
    sequence = jax.random.permutation(stream_key, number_of)
    heavy_load, usual = portions_of(number_of, rows * top, bound, slope, True), portions_of(number_of, rows * top, bound, slope, False)
    places = jnp.arange(number_of)

    def named(lengths, offset_by):
        used = int((lengths > 0).sum())
        fixed = max(1, used // 4)
        moved = fixed + (places - fixed + offset_by * (used - fixed)) % max(1, number_of - fixed)
        return jnp.zeros((number_of,), jnp.int32).at[sequence[jnp.where(places < fixed, places, moved)]].set(jnp.asarray(lengths, jnp.int32))

    lengths = jnp.where(number % 4 == 0, named(heavy_load, number // 4), named(usual, number - number // 4 - 1))
    mixed = jax.random.permutation(jax.random.fold_in(own, 3), number_of)
    source_of, sink = mixed[0:number_of // 2 * 2:2], mixed[1:number_of // 2 * 2:2]
    slack = jnp.minimum(lengths[source_of] - 1, bound - lengths[sink]) // 2
    slack = jnp.where((source_of == sequence[0]) | (sink == sequence[0]) | (lengths[sink] == 0), 0, jnp.maximum(slack, 0))
    moved = jax.random.randint(jax.random.fold_in(own, 4), (number_of // 2,), 0, 1 << 20) % (slack + 1)
    lengths = lengths.at[source_of].add(-moved).at[sink].add(moved)
    labels = jnp.searchsorted(jnp.cumsum(lengths), jnp.arange(rows * top), side="right").astype(jnp.int32)
    listing = labels.reshape(top, rows).T
    listing = listing[jax.random.permutation(jax.random.fold_in(own, 1), rows)]
    offset_by = jax.random.randint(jax.random.fold_in(own, 2), (rows, 1), 0, top)
    return jnp.take_along_axis(listing, (jnp.arange(top)[None, :] + offset_by) % top, axis=1)


def portions_of(number_of, total, most, lean, full):
    portions = [(1 << 20) // math.isqrt(standing ** lean) + 1 for standing in range(1, number_of + 1)]
    largest = most if full else min(most, max(-(-total // number_of), total * portions[0] // sum(portions)))
    least = 1 if total - largest >= number_of - 1 else 0
    counts, rest = [largest] + [least] * (number_of - 1), total - largest - least * (number_of - 1)
    while rest > 0:
        candidates = [i for i in range(1, number_of) if counts[i] < largest] or [i for i in range(1, number_of) if counts[i] < most]
        whole, left = sum([portions[i] for i in candidates]), rest
        for i in candidates:
            addition = min(most - counts[i], max(1, left * portions[i] // whole), rest)
            counts[i] = counts[i] + addition
            rest = rest - addition
    return np.array(counts)


def gaussian(stream_key, extent, scale, reach, split=(), kind=jnp.bfloat16):
    array = jax.random.normal(stream_key, extent, jnp.float32) * scale
    if len(split) > 0:
        array = steps_of(stream_key, extent, split, -0.22, 0.18) * array
    return jnp.clip(array, min=-reach, max=reach).astype(kind)


def setup_inputs(seed: int = 0) -> dict:
    streams_of = jax.random.split(jax.random.key(seed), 8)
    tokens = gaussian(streams_of[0], (TOKENS, MODEL_WIDTH), 1.0, 6.0, ((0, 32), (1, 4)))
    upstream = gaussian(streams_of[1], (TOKENS, MODEL_WIDTH), 1.0, 6.0, ((0, 32), (1, 4)))
    norm_gain = jnp.clip(1.0 + 0.1 * jax.random.normal(streams_of[2], (MODEL_WIDTH,), jnp.float32), 0.5, 1.5).astype(jnp.bfloat16)
    experts_keys = jax.random.split(jax.random.fold_in(streams_of[3], 1), TOKENS // TOK_DEV)
    experts_turns = jax.random.permutation(jax.random.fold_in(streams_of[3], 3), TOKENS // TOK_DEV)
    experts = jax.vmap(lambda own, number: routed_block(jax.random.fold_in(streams_of[3], 2), own, number, TOK_DEV, EXPERTS, TOP, CAP, 2))(experts_keys, experts_turns).reshape((TOKENS, TOP))
    route_weights = jnp.clip(0.049804688 + 0.54785156 * jax.random.uniform(streams_of[4], (TOKENS, TOP), jnp.float32) ** steps_of(streams_of[4], (TOKENS, TOP), ((0, 32),), -0.2, 0.2), 0.049804688, 0.59765625).astype(jnp.bfloat16)
    w_gate_up = gaussian(streams_of[5], (EXPERTS, MODEL_WIDTH, 2, FF), MODEL_WIDTH ** -0.5, 0.109375, ((0, 32), (3, 4)))
    w_down = gaussian(streams_of[6], (EXPERTS, FF, MODEL_WIDTH), FF ** -0.5, 0.15625, ((0, 32), (1, 4)))
    return {"tokens": tokens, "upstream": upstream, "norm_gain": norm_gain, "experts": experts, "route_weights": route_weights, "w_gate_up": w_gate_up, "w_down": w_down}


def expert_terms(x_rows, dy_rows, weight_rows, w_gu, w_dn):
    width = x_rows.shape[1]
    hidden = w_dn.shape[0]
    flat_gu = w_gu.reshape(width, 2 * hidden)
    projected = jnp.dot(x_rows, flat_gu, preferred_element_type=jnp.float32)
    gate_pre = projected[:, :hidden]
    up_pre = projected[:, hidden:]
    sig_gate = jax.nn.sigmoid(1.702 * gate_pre)
    glu_value = gate_pre * sig_gate
    activated = ((up_pre + 1.0) * glu_value).astype(jnp.bfloat16)
    back_proj = lax.dot_general(dy_rows, w_dn, (((1,), (1,)), ((), ())), preferred_element_type=jnp.float32)
    row_weight = weight_rows.astype(jnp.float32)[:, None]
    weight_grad = lax.optimization_barrier(jnp.sum(activated.astype(jnp.float32) * back_proj, axis=1))
    dact = row_weight * back_proj
    dgate_pre = dact * (up_pre + 1.0) * (sig_gate + 1.702 * gate_pre * sig_gate * (1.0 - sig_gate))
    dup_pre = dact * glu_value
    dproj = jnp.concatenate([dgate_pre, dup_pre], axis=1).astype(jnp.bfloat16)
    scaled = (row_weight * activated.astype(jnp.float32)).astype(jnp.bfloat16)
    grad_dn = lax.dot_general(scaled, dy_rows, (((0,), (0,)), ((), ())), preferred_element_type=jnp.float32)
    grad_gu = lax.dot_general(x_rows, dproj, (((0,), (0,)), ((), ())), preferred_element_type=jnp.float32)
    grad_rows = lax.dot_general(dproj, flat_gu, (((1,), (1,)), ((), ())), preferred_element_type=jnp.float32)
    return (grad_gu, grad_dn, grad_rows, weight_grad)

def reference(tokens, upstream, norm_gain, experts, route_weights, w_gate_up, w_down):
    token_single = tokens.astype(jnp.float32)
    gain_single = norm_gain.astype(jnp.float32)
    reciprocal_root_mean = lax.rsqrt(lax.optimization_barrier(jnp.mean(token_single * token_single, axis=1)) + 1e-05)
    standardized_input = token_single * reciprocal_root_mean[:, None]
    normalized_rows = (standardized_input * gain_single[None, :]).astype(jnp.bfloat16)
    pairs = TOKENS * TOP
    block_pairs = experts.reshape(N_SEQ, TOK_DEV * TOP)
    onehot = (block_pairs[:, :, None] == jnp.arange(EXPERTS, dtype=jnp.int32)[None, None, :]).astype(jnp.int32)
    rank = lax.optimization_barrier(jnp.sum((jnp.cumsum(onehot, axis=1) - 1) * onehot, axis=2))
    block_ids = jnp.arange(N_SEQ, dtype=jnp.int32)[:, None]
    position = (block_ids * CAP + rank).reshape(-1).astype(jnp.int32)
    pair_ids = jnp.arange(pairs, dtype=jnp.int32)
    table = jnp.full((EXPERTS, N_SEQ * CAP), pairs, jnp.int32)
    table = table.at[experts.reshape(-1), position].set(pair_ids)
    normed_pad = jnp.concatenate([normalized_rows, jnp.zeros((1, MODEL_WIDTH), jnp.bfloat16)], axis=0)
    upstream_pad = jnp.concatenate([upstream, jnp.zeros((1, MODEL_WIDTH), jnp.bfloat16)], axis=0)
    weights_pad = jnp.concatenate([route_weights.reshape(-1), jnp.zeros((1,), jnp.bfloat16)], axis=0)

    def per_expert(inputs):
        slot_assign, w_gu, w_dn = inputs
        token_rows = (slot_assign // TOP).astype(jnp.int32)
        grad_gu, grad_dn, grad_rows, weight_grad = expert_terms(normed_pad[token_rows], upstream_pad[token_rows], weights_pad[slot_assign], w_gu, w_dn)
        return (grad_gu.astype(jnp.bfloat16), grad_dn.astype(jnp.bfloat16), grad_rows, weight_grad)
    grad_gu, grad_dn, grad_rows, weight_grad = lax.map(per_expert, (table, w_gate_up, w_down))
    flat_table = table.reshape(-1)
    pair_grad = jnp.zeros((pairs + 1, MODEL_WIDTH), jnp.float32).at[flat_table].add(grad_rows.reshape(-1, MODEL_WIDTH))
    normed_gradient = lax.optimization_barrier(jnp.sum(pair_grad[:pairs].reshape(TOKENS, TOP, MODEL_WIDTH), axis=1))
    grad_weights = jnp.zeros((pairs + 1,), jnp.float32).at[flat_table].add(weight_grad.reshape(-1))[:pairs].reshape(TOKENS, TOP)
    correction_term = normed_gradient * gain_single[None, :]
    reduced_statistic = lax.optimization_barrier(jnp.sum(correction_term * standardized_input, axis=1)) / MODEL_WIDTH
    token_gradient = (upstream.astype(jnp.float32) + reciprocal_root_mean[:, None] * (correction_term - standardized_input * reduced_statistic[:, None])).astype(jnp.bfloat16)
    gain_gradient = lax.optimization_barrier(jnp.sum(normed_gradient * standardized_input, axis=0))
    grad_gate_up = grad_gu.reshape(EXPERTS, MODEL_WIDTH, 2, FF)
    return (token_gradient, gain_gradient, grad_weights, grad_gate_up, grad_dn)
```

```python
import functools

import jax
import jax.numpy as jnp
from jax import lax
from jax.experimental import pallas as pl
from jax.experimental.pallas import tpu as pltpu
from jax.sharding import PartitionSpec as P

BF = jnp.bfloat16
F32 = jnp.float32
NT = (((1,), (1,)), ((), ()))
TN = (((0,), (0,)), ((), ()))
HALF = 384


def div(x, d, top):
    mul = (1 << 16) // d + 1
    assert all((v * mul) >> 16 == v // d for v in range(top)) and top * mul < 1 << 31
    return (x * mul) >> 16


def split(x, d, top):
    q = div(x, d, top)
    return q, x - q * d


def dot(a, b, dims=(((1,), (0,)), ((), ()))):
    return lax.dot_general(a, b, dims, preferred_element_type=F32)


def routing(exp_t, experts):
    top, toks = exp_t.shape
    eid = lax.broadcasted_iota(jnp.int32, (experts, toks), 0)
    named = jnp.zeros((experts, toks), F32)
    for k in range(top):
        named = named + jnp.where(exp_t[k : k + 1, :] == eid, 1.0, 0.0)
    before = lax.broadcasted_iota(jnp.int32, (toks, toks), 0) < lax.broadcasted_iota(
        jnp.int32, (toks, toks), 1
    )
    rank = dot(named.astype(BF), jnp.where(before, 1.0, 0.0).astype(BF))
    return jnp.where(named > 0.5, rank, -1.0)


def expert_onehot(rows, per, member, local, experts):
    rid = lax.broadcasted_iota(jnp.int32, (rows, experts), 0)
    eid = lax.broadcasted_iota(jnp.int32, (rows, experts), 1)
    return jnp.where(eid == div(rid, per, rows) * local + member, 1.0, 0.0).astype(BF)


def dispatch_kernel(exp_ref, rw_ref, tok_ref, up_ref, out_ref, *, member, local, experts, cap):
    width, toks = tok_ref.shape
    rows = out_ref.shape[0]
    rest = width - HALF
    exp_t = exp_ref[...]
    ranks = routing(exp_t, experts)
    rw = rw_ref[...].astype(F32)
    eid = lax.broadcasted_iota(jnp.int32, (experts, toks), 0)
    dense = jnp.zeros((experts, toks), F32)
    for k in range(exp_t.shape[0]):
        dense = dense + jnp.where(exp_t[k : k + 1, :] == eid, rw[k : k + 1, :], 0.0)
    pick = expert_onehot(rows, 4 * cap, member, local, experts)
    spread = dot(pick, ranks.astype(BF))
    rid = lax.broadcasted_iota(jnp.int32, (rows, toks), 0)
    _, inside = split(rid, 4 * cap, rows)
    quarter, r = split(inside, cap, 4 * cap)
    hit = spread.astype(jnp.int32) == r
    cat = jnp.concatenate(
        [jnp.where(hit & (quarter == q), 1.0, 0.0).astype(BF) for q in range(4)], axis=1
    )
    pad = jnp.zeros((HALF - rest, toks), BF)
    pieces = []
    for ref in (up_ref, tok_ref):
        pieces.append(ref[:HALF, :])
        pieces.append(jnp.concatenate([ref[HALF:, :], pad], axis=0))
    out = dot(cat, jnp.concatenate(pieces, axis=1), NT)
    weight = jnp.sum(jnp.where(hit, dot(pick, dense.astype(BF)), 0.0), axis=1, keepdims=True)
    lane = lax.broadcasted_iota(jnp.int32, (rows, HALF), 1)
    rid2 = lax.broadcasted_iota(jnp.int32, (rows, HALF), 0)
    _, inside2 = split(rid2, 4 * cap, rows)
    odd = (div(inside2, cap, 4 * cap) & 1) == 1
    out = jnp.where((lane == rest) & odd, weight, out)
    out_ref[...] = out.astype(BF)


def unpack_kernel(got_ref, out_ref, rw_ref, *, cap):
    rows = got_ref.shape[0]
    width, slots = out_ref.shape[1], out_ref.shape[2]
    rest = width - HALF
    rid = lax.broadcasted_iota(jnp.int32, (rows, slots), 0)
    col = lax.broadcasted_iota(jnp.int32, (rows, slots), 1)
    source, inside = split(rid, 4 * cap, rows)
    quarter, r = split(inside, cap, 4 * cap)
    same = col == source * cap + r
    got = got_ref[...]
    for q in range(4):
        sel = jnp.where(same & (quarter == q), 1.0, 0.0).astype(BF)
        part = dot(got, sel, TN)
        if q % 2 == 0:
            out_ref[q // 2, :HALF, :] = part.astype(BF)
        else:
            out_ref[q // 2, HALF:, :] = part[:rest].astype(BF)
            if q == 1:
                rw_ref[...] = part[rest : rest + 8]


def expert_kernel(
    own_ref, prev_ref, next_ref, far_dy_ref, far_x_ref, rw_ref, gain_ref, wgu_ref, wdn_ref,
    gown_ref, gplus_ref, gminus_ref, kplus_ref, kminus_ref, stat_ref, dproj_ref, scaled_ref,
    xn_ref, dy_ref,
    wgu, wdn, x_all, grows, sems, *, parts, eps, member,
):
    width = own_ref.shape[1]
    full = width * parts
    hidden = wdn.shape[0]
    half = width // 2
    z = lax.axis_index("dp")

    def at(k):
        return pl.ds(pl.multiple_of(lax.rem(z + k, parts) * width, 16), width)

    loads = []

    def load(src, dst):
        c = pltpu.make_async_copy(src, dst, sems.at[len(loads)])
        c.start()
        loads.append(c)

    load(wdn_ref.at[member], wdn)
    load(own_ref.at[0], dy_ref.at[at(0)])
    load(prev_ref.at[0], dy_ref.at[at(parts - 1)])
    load(next_ref.at[0], dy_ref.at[at(1)])
    load(far_dy_ref, dy_ref.at[at(2)])
    load(own_ref.at[1], x_all.at[at(0)])
    load(prev_ref.at[1], x_all.at[at(parts - 1)])
    load(next_ref.at[1], x_all.at[at(1)])
    load(far_x_ref, x_all.at[at(2)])
    load(wgu_ref.at[member], wgu)
    for c in loads[:5]:
        c.wait()
    back = dot(wdn[...], dy_ref[...])
    for c in loads[5:9]:
        c.wait()
    chunk = full // 8
    total = jnp.zeros((1, x_all.shape[1]), F32)
    for i in range(8):
        v = x_all[i * chunk : (i + 1) * chunk, :].astype(F32)
        total = total + jnp.sum(v * v, axis=0, keepdims=True)
    inv = lax.rsqrt(total / full + eps)
    for i in range(8):
        s = slice(i * chunk, (i + 1) * chunk)
        v = x_all[s, :].astype(F32) * inv * gain_ref[s, :]
        xn_ref[s, :] = v.astype(BF)
    loads[9].wait()
    proj = dot(wgu[...], xn_ref[...])
    gate, up = proj[:hidden], proj[hidden:]
    rw = rw_ref[0:1, :]
    sig = jax.nn.sigmoid(1.702 * gate)
    glu = gate * sig
    act = ((up + 1.0) * glu).astype(BF).astype(F32)
    wgrad = jnp.sum(act * back, axis=0, keepdims=True)
    dact = rw * back
    dgate = dact * (up + 1.0) * (sig + 1.702 * gate * sig * (1.0 - sig))
    dproj_ref[:hidden, :] = dgate.astype(BF)
    dproj_ref[hidden:, :] = (dact * glu).astype(BF)
    scaled_ref[...] = (rw * act).astype(BF)
    cs = jnp.zeros((1, x_all.shape[1]), F32)
    dproj = dproj_ref[...]
    for i in range(parts):
        s = slice(i * width, (i + 1) * width)
        g = dot(wgu[:, s], dproj, TN)
        grows[s, :] = g.astype(BF)
        cs = cs + jnp.sum(g * (x_all[s, :].astype(F32) * gain_ref[s, :]), axis=0, keepdims=True)
    cs = cs * inv
    gown_ref[...] = grows[at(0), :]
    far = grows[at(2), :]
    plus = grows[at(1), :]
    minus = grows[at(parts - 1), :]
    gplus_ref[:half, :] = far[:half]
    gplus_ref[half:, :] = plus[half:]
    gminus_ref[:half, :] = far[half:]
    gminus_ref[half:, :] = minus[:half]
    kplus_ref[...] = plus[:half]
    kminus_ref[...] = minus[half:]
    stat_ref[0:1, :] = wgrad
    stat_ref[1:2, :] = cs
    stat_ref[2:3, :] = inv
    stat_ref[3:8, :] = jnp.zeros((5, inv.shape[1]), F32)


def weight_grad_kernel(dproj_ref, scaled_ref, xn_ref, dy_ref, *rest):
    ggu_ref, gdn_ref = rest[-2:]
    ggu_ref[0] = dot(dproj_ref[...], xn_ref[...], NT).astype(BF)
    gdn_ref[0] = dot(scaled_ref[...], dy_ref[...], NT).astype(BF)


def pack_kernel(
    own_ref, gown_ref, fromp_ref, fromm_ref, fwdp_ref, fwdm_ref, st0, st1, st2, st3, gp_ref,
    out_ref, gpo_ref, *, cap, per, last,
):
    width, slots = gown_ref.shape
    half = width // 2
    rest = width - HALF
    total = gown_ref[...].astype(F32) + jnp.concatenate(
        [
            fromm_ref[half:, :].astype(F32) + fwdp_ref[...].astype(F32),
            fromp_ref[half:, :].astype(F32) + fwdm_ref[...].astype(F32),
        ],
        axis=0,
    )
    inv = st0[2:3, :]
    prod = total * (own_ref[0].astype(F32) * inv)
    gp = lax.dot_general(
        jnp.ones((8, slots), F32), prod, NT, precision=lax.Precision.HIGHEST,
        preferred_element_type=F32,
    )
    gp = gp + gp_ref[...]
    gpo_ref[...] = gp
    stat = st0[0:2, :] + st1[0:2, :] + st2[0:2, :] + st3[0:2, :]
    hi = stat.astype(BF)
    lo = (stat - hi.astype(F32)).astype(BF)
    low = total[:HALF].astype(BF)
    high = jnp.concatenate(
        [
            total[HALF:],
            hi.astype(F32),
            lo.astype(F32),
            jnp.zeros((HALF - rest - 4, slots), F32),
        ],
        axis=0,
    ).astype(BF)
    rows = out_ref.shape[0]
    rid = lax.broadcasted_iota(jnp.int32, (rows, slots), 0)
    col = lax.broadcasted_iota(jnp.int32, (rows, slots), 1)
    dest, inside = split(rid, per, rows)
    h, r = split(inside, cap, per)
    same = col == dest * cap + r
    out = dot(jnp.where(same & (h == 0), 1.0, 0.0).astype(BF), low, NT)
    out = out + dot(jnp.where(same & (h == 1), 1.0, 0.0).astype(BF), high, NT)
    if last:
        ghi = gp[0:1, :].astype(BF).astype(F32)
        glo = gp[0:1, :] - ghi
        inside_l = split(lax.broadcasted_iota(jnp.int32, (rows, HALF), 0), per, rows)[1]
        pad = jnp.zeros((1, HALF - rest), F32)
        for i, v in enumerate((ghi, glo)):
            out = jnp.where(inside_l == 2 * cap + 2 * i, v[:, :HALF], out)
            out = jnp.where(
                inside_l == 2 * cap + 2 * i + 1, jnp.concatenate([v[:, HALF:], pad], axis=1), out
            )
    out_ref[...] = out.astype(BF)


def final_kernel(
    exp_ref, tok_ref, up_ref, gain_ref, ss_ref, ra_ref, rb_ref, tg_ref, gw_ref, gg_ref,
    *, pers, local, experts, cap, full, eps,
):
    width, toks = tok_ref.shape
    rest = width - HALF
    exp_t = exp_ref[...]
    ranks = routing(exp_t, experts).astype(BF)
    acc = jnp.zeros((HALF, 2 * toks), F32)
    dense = jnp.zeros((experts, toks), F32)
    for member, (ref, per) in enumerate(zip((ra_ref, rb_ref), pers)):
        rows = ref.shape[0]
        pick = expert_onehot(rows, per, member, local, experts)
        spread = dot(pick, ranks).astype(jnp.int32)
        rid = lax.broadcasted_iota(jnp.int32, (rows, toks), 0)
        _, inside = split(rid, per, rows)
        h, r = split(inside, cap, per)
        hit = spread == r
        m0 = jnp.where(hit & (h == 0), 1.0, 0.0).astype(BF)
        on1 = hit & (h == 1)
        m1 = jnp.where(on1, 1.0, 0.0).astype(BF)
        got = ref[...]
        acc = acc + dot(got, jnp.concatenate([m0, m1], axis=1), TN)
        stat = got[:, 256:].astype(F32)
        for j in (0, 2):
            value = stat[:, rest - 256 + j : rest - 256 + j + 1]
            dense = dense + dot(pick, jnp.where(on1, value, 0.0).astype(BF), TN)
    eid = lax.broadcasted_iota(jnp.int32, (experts, toks), 0)
    for k in range(exp_t.shape[0]):
        gw_ref[k : k + 1, :] = jnp.sum(
            jnp.where(exp_t[k : k + 1, :] == eid, dense, 0.0), axis=0, keepdims=True
        )
    inv = lax.rsqrt(ss_ref[...] / full + eps)
    high = acc[:, toks:]
    c = (high[rest + 1 : rest + 2, :] + high[rest + 3 : rest + 4, :]) / full
    dn = jnp.concatenate([acc[:, :toks], high[:rest]], axis=0)
    u = dn * gain_ref[...]
    xhat = tok_ref[...].astype(F32) * inv
    tg_ref[...] = (up_ref[...].astype(F32) + inv * (u - xhat * c)).astype(BF)
    per = pers[1]
    rows = rb_ref.shape[0]
    kid = lax.broadcasted_iota(jnp.int32, (8, rows), 0)
    ins = split(lax.broadcasted_iota(jnp.int32, (8, rows), 1), per, rows)[1]
    want = ((kid == 0) & ((ins == 2 * cap) | (ins == 2 * cap + 2))) | (
        (kid == 1) & ((ins == 2 * cap + 1) | (ins == 2 * cap + 3))
    )
    g = dot(jnp.where(want, 1.0, 0.0).astype(BF), rb_ref[...])
    gg_ref[...] = jnp.concatenate([g[0:1, :], g[1:2, :rest]], axis=1)


VMEM = pltpu.VMEM


def call(kernel, outs, args, scratch=(), anys=(), out_anys=(), flops=0, aliases=None, moved=0):
    vm = pl.BlockSpec(memory_space=VMEM)
    hb = pl.BlockSpec(memory_space=pl.ANY)
    return pl.pallas_call(
        kernel,
        out_shape=outs,
        in_specs=[hb if i in anys else vm for i in range(len(args))],
        out_specs=[hb if i in out_anys else vm for i in range(len(outs))],
        scratch_shapes=list(scratch),
        input_output_aliases=aliases or {},
        compiler_params=pltpu.CompilerParams(vmem_limit_bytes=60 << 20),
        cost_estimate=pl.CostEstimate(flops=flops, transcendentals=0, bytes_accessed=moved),
    )(*args)


def body(tokens, upstream, norm_gain, experts, route_weights, w_gate_up, w_down):
    S = jax.ShapeDtypeStruct
    parts = lax.axis_size("dp")
    seqs = lax.axis_size("seq")
    toks, width = tokens.shape
    full = width * parts
    top = experts.shape[1]
    local = w_gate_up.shape[0]
    hidden = w_down.shape[1]
    total = local * seqs
    cap = toks * top * 3 // (2 * total)
    slots = seqs * cap
    eps = 1e-05
    tok_t, up_t = tokens.T, upstream.T
    exp_t, rw_t = experts.T, route_weights.T
    wgu = jnp.transpose(w_gate_up, (0, 2, 3, 1)).reshape(local, 2 * hidden, full)
    gain = norm_gain.astype(F32)[:, None]
    gain_own = lax.dynamic_slice_in_dim(gain, lax.axis_index("dp") * width, width, 0)
    fwd = [(i, (i + 1) % parts) for i in range(parts)]
    bwd = [(i, (i - 1) % parts) for i in range(parts)]
    opp = [(i, (i + 2) % parts) for i in range(parts)]

    def perm(x, p):
        return lax.ppermute(x, "dp", p)

    per = 4 * cap
    shards, weights = [], []
    for m in range(local):
        send = call(
            functools.partial(
                dispatch_kernel, member=m, local=local, experts=total, cap=cap
            ),
            [S((seqs * per, HALF), BF)],
            (exp_t, rw_t, tok_t, up_t),
            flops=2 * seqs * per * HALF * 4 * toks,
        )[0]
        got = lax.all_to_all(send.reshape(seqs, per, HALF), "seq", 0, 0, tiled=True)
        shard, rw = call(
            functools.partial(unpack_kernel, cap=cap),
            [S((2, width, slots), BF), S((8, slots), F32)],
            (got.reshape(seqs * per, HALF),),
            flops=2 * seqs * per * HALF * 4 * slots,
        )
        shards.append(shard)
        weights.append(rw)
    sums = lax.psum(jnp.sum(jnp.square(tok_t.astype(F32)), axis=0, keepdims=True), "dp")
    gathered = []
    for m in range(local):
        a = perm(shards[m], fwd)
        b = perm(shards[m], bwd)
        far_dy = perm(a[0], fwd)
        far_x = perm(b[1], bwd)
        gathered.append((shards[m], a, b, far_dy, far_x))
    ggu = gdn = None
    gp = jnp.zeros((8, width), F32)
    backs = []
    half = width // 2
    pers = (2 * cap, -(-(2 * cap + 4) // 8) * 8)
    for m in range(local):
        blk = S((width, slots), BF)
        hb = S((half, slots), BF)
        outs = call(
            functools.partial(expert_kernel, parts=parts, eps=eps, member=m),
            [
                blk, blk, blk, hb, hb, S((8, slots), F32), S((2 * hidden, slots), BF),
                S((hidden, slots), BF), S((full, slots), BF), S((full, slots), BF),
            ],
            (*gathered[m], weights[m], gain, wgu, w_down),
            scratch=[
                VMEM((2 * hidden, full), BF), VMEM((hidden, full), BF), VMEM((full, slots), BF),
                VMEM((full, slots), BF), pltpu.SemaphoreType.DMA((10,)),
            ],
            anys=(0, 1, 2, 3, 4, 7, 8),
            flops=2 * slots * full * hidden * 5,
        )
        gown, gplus, gminus, kplus, kminus, stat, dproj, scaled, xn, dy = outs
        x1 = perm(gplus, fwd)
        y1 = perm(gminus, bwd)
        s1, s2, s3 = perm(stat, fwd), perm(stat, bwd), perm(stat, opp)
        f2 = perm(kplus + x1[:half], fwd)
        h2 = perm(kminus + y1[:half], bwd)
        sh = [S((local, 2 * hidden, full), BF), S((local, hidden, full), BF)]
        blocks = [
            pl.BlockSpec((1, 2 * hidden, full), lambda i, m=m: (m, 0, 0)),
            pl.BlockSpec((1, hidden, full), lambda i, m=m: (m, 0, 0)),
        ]
        ins = [dproj, scaled, xn, dy]
        specs = [pl.BlockSpec(v.shape, lambda i: (0, 0)) for v in ins]
        if m:
            ins += [ggu, gdn]
            specs += [pl.BlockSpec(memory_space=pl.ANY)] * 2
        ggu, gdn = pl.pallas_call(
            weight_grad_kernel,
            grid=(1,),
            out_shape=sh,
            in_specs=specs,
            out_specs=blocks,
            input_output_aliases={4: 0, 5: 1} if m else {},
            compiler_params=pltpu.CompilerParams(vmem_limit_bytes=60 << 20),
            cost_estimate=pl.CostEstimate(
                flops=6 * slots * full * hidden, transcendentals=0, bytes_accessed=0
            ),
        )(*ins)
        send, gp = call(
            functools.partial(pack_kernel, cap=cap, per=pers[m], last=m == local - 1),
            [S((seqs * pers[m], HALF), BF), S((8, width), F32)],
            (shards[m][1:2], gown, x1, y1, f2, h2, stat, s1, s2, s3, gp),
            flops=4 * seqs * pers[m] * HALF * slots,
        )
        back = lax.all_to_all(send.reshape(seqs, pers[m], HALF), "seq", 0, 0, tiled=True)
        backs.append(back.reshape(seqs * pers[m], HALF))
    tg, gw, gg = call(
        functools.partial(
            final_kernel, pers=pers, local=local, experts=total, cap=cap, full=full, eps=eps
        ),
        [S((width, toks), BF), S((top, toks), F32), S((1, width), F32)],
        (exp_t, tok_t, up_t, gain_own, sums, *backs),
        flops=2 * seqs * per * HALF * toks * 4,
    )
    ggu = jnp.transpose(ggu.reshape(local, 2, hidden, full), (0, 3, 1, 2))
    return tg.T, gg.reshape(-1), gw.T, ggu, gdn


def solution(mesh):
    in_specs = (
        P("seq", "dp"),
        P("seq", "dp"),
        P(),
        P("seq", None),
        P("seq", None),
        P("seq", None, None, "dp"),
        P("seq", "dp", None),
    )
    out_specs = (
        P("seq", "dp"),
        P("dp"),
        P("seq", None),
        P("seq", None, None, "dp"),
        P("seq", "dp", None),
    )
    return jax.shard_map(body, mesh=mesh, in_specs=in_specs, out_specs=out_specs, check_vma=False)
```
